768 devices in a mesh: pts: 64 (over y, x, core), bins: 12 (over z).
Axes of the slice: x: 4, y: 8, z: 12, core: 2. Of those that a mesh axis runs over, the one named last changes fastest.
Arguments:
- spectrum: bfloat16 [1296, 256, 1536], P('bins', 'pts'), may hold values from 0.049804688 to 4
- courant: float32 [1296, 2], replicated, may hold values from 0.05 to 0.45
- upwind: int32 [1296, 2], replicated, may hold values from 0 to 1
- coupling: bfloat16 [1296, 1296], replicated, may hold values from -0.15625 to 0.15625
- sea: int32 [256, 1536], P('pts'), may hold values 0 or 1
- owner: int32 [64, 12, 512, 1], P('pts', 'bins'), may hold values from 0 to 63; in each aligned block of 512 rows (0 to 511, 512 to 1023, ..., all dimensions but the last counted through in order) at most 16 rows name the same one
Outputs:
- owner_rows: bfloat16 [64, 12, 1024, 1296], P('pts', 'bins')
The draws below stay inside these ranges and needn't reach their ends.
Inputs may be any that keep to these rules, and one draw needn't show every extreme that they name: Among the 512 points of one block, at most 16 name the same owner, and in every draw some owner is named by exactly 16 points of some block.
All inputs are finite; a program needn't handle non-finite values. No bound on the sum of `sea` on one device may be relied on, other than what follows from the above.
Results may differ from the reference program's by a relative error of at most 0.0049.
Values may be sent and summed in bfloat16 or wider, within the bound.
A program may use at most 32 MiB of HBM per device.

```python
import math
import jax
import jax.numpy as jnp
import numpy as np
from jax import lax

LON_DEV = 4
LAT_DEV = 128
BINS = 1296
NLON = 256
NLAT = 1536
PB = 512
CAP = 16
N_PTS = 64
N_BINS = 12


def set_ends(drawn, stream_key, smallest, high):
    longest = drawn.shape.index(max(drawn.shape))
    spots = []
    for shift in (0, 1):
        where = [jax.random.randint(jax.random.fold_in(stream_key, axis), (), 0, length) for axis, length in enumerate(drawn.shape)]
        where[longest] = (where[longest] + shift) % drawn.shape[longest]
        spots.append(tuple(where))
    return drawn.at[spots[0]].set(smallest).at[spots[1]].set(high)


def block_scale(key, dims, cuts, low, top_value):
    def one(position, shards_of):
        heights = jax.random.uniform(jax.random.fold_in(jax.random.fold_in(key, 6), position), (shards_of,), jnp.float32, low / len(cuts), top_value / len(cuts))
        return jnp.repeat(jnp.exp(heights), dims[position] // shards_of).reshape((-1,) + (1,) * (len(dims) - position - 1))

    gain = one(*cuts[0])
    for cut in cuts[1:]:
        gain = gain * one(*cut)
    return gain


def shared_out(stream_key, own, number, rows, number_of, top, reach, slope):
    order = jax.random.permutation(stream_key, number_of)
    crowded, common = shares(number_of, rows * top, reach, slope, True), shares(number_of, rows * top, reach, slope, False)
    places = jnp.arange(number_of)

    def named(sizes, offset_by):
        used = int((sizes > 0).sum())
        fixed = max(1, used // 4)
        moved = fixed + (places - fixed + offset_by * (used - fixed)) % max(1, number_of - fixed)
        return jnp.zeros((number_of,), jnp.int32).at[order[jnp.where(places < fixed, places, moved)]].set(jnp.asarray(sizes, jnp.int32))

    sizes = jnp.where(number % 4 == 0, named(crowded, number // 4), named(common, number - number // 4 - 1))
    mixed = jax.random.permutation(jax.random.fold_in(own, 3), number_of)
    giver, receiver = mixed[0:number_of // 2 * 2:2], mixed[1:number_of // 2 * 2:2]
    room = jnp.minimum(sizes[giver] - 1, reach - sizes[receiver]) // 2
    room = jnp.where((giver == order[0]) | (receiver == order[0]) | (sizes[receiver] == 0), 0, jnp.maximum(room, 0))
    moved = jax.random.randint(jax.random.fold_in(own, 4), (number_of // 2,), 0, 1 << 20) % (room + 1)
    sizes = sizes.at[giver].add(-moved).at[receiver].add(moved)
    items = jnp.searchsorted(jnp.cumsum(sizes), jnp.arange(rows * top), side="right").astype(jnp.int32)
    grid = items.reshape(top, rows).T
    grid = grid[jax.random.permutation(jax.random.fold_in(own, 1), rows)]
    offset_by = jax.random.randint(jax.random.fold_in(own, 2), (rows, 1), 0, top)
    return jnp.take_along_axis(grid, (jnp.arange(top)[None, :] + offset_by) % top, axis=1)


def shares(number_of, total, limit, skew, full):
    loads = [(1 << 20) // math.isqrt(rank ** skew) + 1 for rank in range(1, number_of + 1)]
    largest = limit if full else min(limit, max(-(-total // number_of), total * loads[0] // sum(loads)))
    least = 1 if total - largest >= number_of - 1 else 0
    holding, surplus = [largest] + [least] * (number_of - 1), total - largest - least * (number_of - 1)
    while surplus > 0:
        candidates = [i for i in range(1, number_of) if holding[i] < largest] or [i for i in range(1, number_of) if holding[i] < limit]
        pool, budget = sum([loads[i] for i in candidates]), surplus
        for i in candidates:
            addition = min(limit - holding[i], max(1, budget * loads[i] // pool), surplus)
            holding[i] = holding[i] + addition
            surplus = surplus - addition
    return np.array(holding)


def scatter_about(stream_key, dims, spread, bound, held_as=jnp.bfloat16):
    return jnp.clip(spread * jax.random.normal(stream_key, dims, jnp.float32), -bound, bound).astype(held_as)


def setup_inputs(seed: int = 0) -> dict:
    seeds = jax.random.split(jax.random.key(seed), 7)
    spectrum = jnp.clip(jnp.exp(math.log(4.0) - 4.3859405 * jax.random.uniform(seeds[0], (BINS, NLON, NLAT), jnp.float32) ** block_scale(seeds[0], (BINS, NLON, NLAT), ((0, 12), (1, 64)), -0.2, 0.2)), 0.049804688, 4.0).astype(jnp.bfloat16)
    courant = jnp.clip(jax.random.uniform(seeds[1], (BINS, 2), jnp.float32, 0.05, 0.45), 0.05, 0.45)
    upwind = set_ends(jax.random.randint(seeds[2], (BINS, 2), 0, 2), jax.random.fold_in(seeds[2], 1), 0, 1).astype(jnp.int32)
    coupling = scatter_about(seeds[3], (BINS, BINS), BINS ** -0.5, 0.15625)
    sea = set_ends((jax.random.randint(seeds[4], (NLON, NLAT), 0, 10) < 7).astype(jnp.int32), jax.random.fold_in(seeds[4], 1), 0, 1)
    owner_keys = jax.random.split(jax.random.fold_in(seeds[5], 1), N_PTS * N_BINS * PB // PB)
    owner_turns = jax.random.permutation(jax.random.fold_in(seeds[5], 3), N_PTS * N_BINS * PB // PB)
    owner = jax.vmap(lambda own, number: shared_out(jax.random.fold_in(seeds[5], 2), own, number, PB, N_PTS, 1, CAP, 2))(owner_keys, owner_turns).reshape((N_PTS, N_BINS, PB, 1))
    return dict(spectrum=spectrum, courant=courant, upwind=upwind, coupling=coupling, sea=sea, owner=owner)


def reference(spectrum, courant, upwind, coupling, sea, owner):
    sea_mask = sea.astype(jnp.float32)
    masked = spectrum.astype(jnp.float32) * sea_mask[None]
    padded = jnp.pad(masked, ((0, 0), (1, 1), (1, 1)))
    center = padded[:, 1:-1, 1:-1]
    donor_x = jnp.where(upwind[:, 0][:, None, None] == 0, padded[:, :-2, 1:-1], padded[:, 2:, 1:-1])
    donor_y = jnp.where(upwind[:, 1][:, None, None] == 0, padded[:, 1:-1, :-2], padded[:, 1:-1, 2:])
    moved = center - courant[:, 0][:, None, None] * (center - donor_x) - courant[:, 1][:, None, None] * (center - donor_y)
    propagated = (moved * sea_mask[None]).astype(jnp.bfloat16)
    point_major = jnp.transpose(propagated, (1, 2, 0))

    def source_row(inputs):
        point_rows, weights = inputs
        energy = jnp.mean(point_rows.astype(jnp.float32), axis=1)
        coupled = jnp.dot(point_rows, coupling, preferred_element_type=jnp.float32)
        return (weights[:, None] * (point_rows.astype(jnp.float32) + coupled) / (1.0 + energy)[:, None]).astype(jnp.bfloat16)

    updated = lax.map(source_row, (point_major, sea_mask))
    blocks = updated.reshape(N_PTS, LON_DEV, N_BINS, LAT_DEV, BINS)
    blocks = jnp.transpose(blocks, (0, 2, 1, 3, 4)).reshape(N_PTS, N_BINS, PB, BINS)
    target = owner[..., 0].astype(jnp.int32)
    onehot = (target[..., None] == jnp.arange(N_PTS, dtype=jnp.int32)).astype(jnp.int32)
    slot_rank = jnp.sum(jnp.cumsum(onehot, axis=2) * onehot, axis=-1) - 1
    source = jnp.arange(N_PTS, dtype=jnp.int32)[:, None, None]
    slot_row = source * CAP + slot_rank
    bin_index = jnp.broadcast_to(jnp.arange(N_BINS, dtype=jnp.int32)[None, :, None], target.shape)
    result = jnp.zeros((N_PTS, N_BINS, N_PTS * CAP, BINS), jnp.bfloat16)
    return result.at[target, bin_index, slot_row].set(blocks)
```

```python
import functools

import jax
import jax.numpy as jnp
from jax import lax
from jax.experimental import pallas as pl
from jax.experimental.pallas import tpu as pltpu
from jax.sharding import PartitionSpec as P

MESH = pl.DeviceIdType.MESH
BF16, F32 = jnp.bfloat16, jnp.float32
NT = (((1,), (1,)), ((), ()))
LANES = 128


def dot(a, b, dims=None):
    if dims is None:
        return jnp.dot(a, b, preferred_element_type=F32)
    return lax.dot_general(a, b, dims, preferred_element_type=F32)


def zigzag(count, step):
    return (count // 2 + ((step + 1) // 2) * (1 - 2 * (step % 2))) % count


def pts_peer(me, count, step):
    if count != 64:
        return (me + 1 + step) % count
    y = (me // 8 + zigzag(8, step // 8)) % 8
    x = ((me // 2) % 4 + zigzag(4, (step // 2) % 4)) % 4
    core = (me % 2 + 1 - step % 2) % 2
    return y * 8 + x * 2 + core


def bins_peer(me, count, step):
    return (me + zigzag(count, step)) % count


def round_bins(padded):
    sizes, at, out = [16], 16, [(0, 16)]
    while at < padded:
        size = min(32, padded - at)
        out.append((at, size))
        at += size
    return out


def kernel(dims, masked, courant, upwind, sea, owner, coupling, out, *scratch):
    np_, nb, lb, rounds, lon, lc, cap, slots, bins = dims
    nr = len(rounds)
    (hbuf, coef, sel, dbuf, acc, hss, hrs, zss, zrs, xss, xrs), rest = scratch[:11], scratch[11:]
    send, got, gath, recv, wmat, imat = [rest[k * nr:(k + 1) * nr] for k in range(6)]
    me = lax.axis_index("pts")
    mz = lax.axis_index("bins")
    up, down = (me + 1) % np_, (me + np_ - 1) % np_
    lat = masked.shape[2]
    pts = lon * lc
    tiles = 4
    mt = slots // tiles

    barrier = pltpu.get_barrier_semaphore()

    @pl.loop(0, np_ - 1)
    def _(k):
        pl.semaphore_signal(barrier, inc=1, device_id={"pts": pts_peer(me, np_, k)}, device_id_type=MESH)

    @pl.loop(0, nb - 1)
    def _(k):
        pl.semaphore_signal(barrier, inc=1, device_id={"bins": bins_peer(mz, nb, k)}, device_id_type=MESH)

    first = mz * lb
    rows = lax.broadcasted_iota(jnp.int32, (coef.shape[0], bins), 0)
    cols = lax.broadcasted_iota(jnp.int32, (coef.shape[0], bins), 1)
    pick = jnp.where((rows < lb) & (cols == rows + first), 1.0, 0.0).astype(F32)
    table = jnp.concatenate(
        [courant[...], upwind[...].astype(F32), jnp.zeros((4, bins), F32)], axis=0
    )
    coef[:, 0:8] = lax.dot_general(
        pick, table, NT, precision=lax.Precision.HIGHEST, preferred_element_type=F32
    )

    ids = lax.broadcasted_iota(jnp.int32, (np_, lc), 0)
    named = jnp.concatenate(
        [jnp.where(ids == owner[i:i + 1, :], 1.0, 0.0) for i in range(lon)], axis=1
    )
    before = lax.broadcasted_iota(jnp.int32, (pts, pts), 0)
    after = lax.broadcasted_iota(jnp.int32, (pts, pts), 1)
    upper = jnp.where(before <= after, 1.0, 0.0).astype(BF16)
    counts = dot(named.astype(BF16), upper)
    rank = jnp.sum(counts * named, axis=0, keepdims=True) - 1.0
    column = pl.multiple_of(mz * lc, LANES)
    for i in range(lon):
        slot = owner[i:i + 1, :].astype(F32) * float(cap) + rank[:, i * lc:(i + 1) * lc]
        weight = sea[i:i + 1, pl.ds(column, lc)].astype(F32)
        row = lax.broadcasted_iota(jnp.int32, (slots, lc), 0).astype(F32)
        sel[:, i * lc:(i + 1) * lc] = jnp.where(row == slot, weight, 0.0).astype(BF16)

    pl.semaphore_wait(barrier, np_ - 1 + nb - 1)

    for r, (q0, qn) in enumerate(rounds):
        for row, there, side in ((lon - 1, up, 0), (0, down, 1)):
            pltpu.make_async_remote_copy(
                src_ref=masked.at[row, pl.ds(q0, qn)],
                dst_ref=hbuf.at[side, pl.ds(q0, qn)],
                send_sem=hss.at[r],
                recv_sem=hrs.at[r],
                device_id={"pts": there},
                device_id_type=MESH,
            ).start()

    low_on = jnp.where(me > 0, 1.0, 0.0).astype(F32)
    high_on = jnp.where(me < np_ - 1, 1.0, 0.0).astype(F32)
    lane = lax.broadcasted_iota(jnp.int32, (16, lat), 1)
    for r, (q0, qn) in enumerate(rounds):
        span = pl.ds(q0, qn)
        pltpu.make_async_copy(hbuf.at[:, span], hbuf.at[:, span], hrs.at[r]).wait()
        for h in range(qn // 16):
            a0 = q0 + 16 * h
            at = pl.ds(a0, 16)
            cx, cy = coef[at, 0:1], coef[at, 1:2]
            ux, uy = coef[at, 2:3], coef[at, 3:4]
            lines = [hbuf[0, at, :].astype(F32) * low_on]
            lines += [masked[i, at, :].astype(F32) for i in range(lon)]
            lines += [hbuf[1, at, :].astype(F32) * high_on]
            for i in range(lon):
                center = lines[i + 1]
                donor_x = jnp.where(ux == 0.0, lines[i], lines[i + 2])
                lower = jnp.where(lane == 0, 0.0, pltpu.roll(center, 1, 1))
                higher = jnp.where(lane == lat - 1, 0.0, pltpu.roll(center, lat - 1, 1))
                donor_y = jnp.where(uy == 0.0, lower, higher)
                moved = center - cx * (center - donor_x) - cy * (center - donor_y)
                moved = (moved * sea[i:i + 1, :].astype(F32)).astype(BF16)
                for j in range(nb):
                    send[r][j, i, pl.ds(16 * h, 16), :] = moved[:, j * lc:(j + 1) * lc]

        @pl.loop(0, nb - 1)
        def _(k):
            there = bins_peer(mz, nb, k)
            pltpu.make_async_remote_copy(
                src_ref=send[r].at[there],
                dst_ref=got[r].at[mz],
                send_sem=zss.at[r],
                recv_sem=zrs.at[r],
                device_id={"bins": there},
                device_id_type=MESH,
            ).start()

        pltpu.make_async_copy(send[r].at[mz], got[r].at[mz], zrs.at[r]).start()

    def select(r):
        qn = rounds[r][1]
        pltpu.make_async_copy(send[r], got[r], zrs.at[r]).wait()
        width = nb * qn
        block = jnp.concatenate(
            [got[r][:, i].reshape(width, lc) for i in range(lon)], axis=1
        )

        @pl.loop(0, tiles)
        def _(m):
            part = sel[pl.ds(pl.multiple_of(m * mt, mt), mt), :]
            block = jnp.concatenate(
                [got[r][:, i].reshape(width, lc) for i in range(lon)], axis=1
            )
            rows = dot(part, block, NT).astype(BF16)
            gath[r][pl.ds(m * (np_ // tiles), np_ // tiles), :, 0:width] = rows.reshape(
                np_ // tiles, cap, width
            )

        @pl.loop(0, np_ - 1)
        def _(k):
            there = pts_peer(me, np_, k)
            pltpu.make_async_remote_copy(
                src_ref=gath[r].at[there],
                dst_ref=recv[r].at[me],
                send_sem=xss.at[r],
                recv_sem=xrs.at[r],
                device_id={"pts": there},
                device_id_type=MESH,
            ).start()

        pltpu.make_async_copy(gath[r].at[me], recv[r].at[me], xrs.at[r]).start()

    ot = dbuf.shape[1] // LANES

    def prepare(r):
        q0, qn = rounds[r]
        width = nb * qn
        full = wmat[r].shape[0]

        def bin_of(k):
            q = k % qn + q0
            return jnp.where(q < lb, (k // qn) * lb + q, -1)

        k = lax.broadcasted_iota(jnp.int32, (width, bins), 0)
        n = lax.broadcasted_iota(jnp.int32, (width, bins), 1)
        order = jnp.where(n == bin_of(k), 1.0, 0.0).astype(BF16)
        dbuf[0:width, 0:bins] = dot(order, coupling[...]).astype(BF16)
        if dbuf.shape[1] > bins:
            dbuf[0:width, bins:] = jnp.zeros((width, dbuf.shape[1] - bins), BF16)
        e0 = lax.broadcasted_iota(jnp.int32, (LANES, LANES), 0)
        e1 = lax.broadcasted_iota(jnp.int32, (LANES, LANES), 1)
        eye = jnp.where(e0 == e1, 1.0, 0.0).astype(BF16)
        for t in range(ot):
            wmat[r][t * LANES:(t + 1) * LANES, :] = dot(
                eye, dbuf[0:width, t * LANES:(t + 1) * LANES], NT
            ).astype(BF16)
        wmat[r][bins:bins + 8, :] = jnp.ones((8, width), BF16)
        n = lax.broadcasted_iota(jnp.int32, (full, width), 0)
        k = lax.broadcasted_iota(jnp.int32, (full, width), 1)
        imat[r][...] = jnp.where(n == bin_of(k), 1.0, 0.0).astype(BF16)

    def couple(r):
        width = nb * rounds[r][1]
        pltpu.make_async_copy(gath[r], recv[r], xrs.at[r]).wait()

        @pl.loop(0, tiles)
        def _(m):
            rows = recv[r][pl.ds(m * (np_ // tiles), np_ // tiles), :, 0:width].reshape(mt, width)
            total = dot(wmat[r][0:bins + 8, :], rows, NT) + dot(imat[r][0:bins + 8, :], rows, NT)
            if r > 0:
                total = total + acc[m]
            if r < nr - 1:
                acc[m] = total
            else:
                scale = 1.0 / (1.0 + total[bins:bins + 1, :] / float(bins))
                out[:, pl.ds(pl.multiple_of(m * mt, mt), mt)] = (total[0:bins] * scale).astype(BF16)

    select(0)
    for r in range(nr):
        prepare(r)
        if r + 1 < nr:
            select(r + 1)
    for r in range(nr):
        couple(r)
    for r, (q0, qn) in enumerate(rounds):
        span = pl.ds(q0, qn)
        pltpu.make_async_copy(hbuf.at[:, span], hbuf.at[:, span], hss.at[r]).wait()
        pltpu.make_async_copy(send[r].at[pl.ds(0, nb - 1)], got[r].at[pl.ds(0, nb - 1)], zss.at[r]).wait()
        pltpu.make_async_copy(gath[r].at[pl.ds(0, np_ - 1)], recv[r].at[pl.ds(0, np_ - 1)], xss.at[r]).wait()


def local(spectrum, courant, upwind, coupling, sea, owner):
    lb, lon, lat = spectrum.shape
    np_, nb = lax.axis_size("pts"), lax.axis_size("bins")
    bins = coupling.shape[0]
    lc = lat // nb
    pts = lon * lc
    cap = max(2, (2 * pts + np_ - 1) // np_)
    slots = np_ * cap
    padded = -(-lb // 16) * 16
    rounds = round_bins(padded)
    nr = len(rounds)
    masked = jnp.transpose(spectrum * sea.astype(BF16)[None], (1, 0, 2))
    masked = jnp.pad(masked, ((0, 0), (0, padded - lb), (0, 0)))
    wide = [-(-nb * q // LANES) * LANES for _, q in rounds]
    full = -(-(bins + 8) // LANES) * LANES
    dims = (np_, nb, lb, rounds, lon, lc, cap, slots, bins)
    scratch = [
        pltpu.VMEM((2, padded, lat), BF16),
        pltpu.VMEM((padded, LANES), F32),
        pltpu.VMEM((slots, pts), BF16),
        pltpu.VMEM((nb * 32, full), BF16),
        pltpu.VMEM((4, bins + 8, slots // 4), F32),
    ]
    scratch += [pltpu.SemaphoreType.DMA((nr,))] * 6
    scratch += [pltpu.VMEM((nb, lon, q, lc), BF16) for _, q in rounds] * 2
    scratch += [pltpu.VMEM((np_, cap, w), BF16) for w in wide] * 2
    scratch += [pltpu.VMEM((full, nb * q), BF16) for _, q in rounds] * 2
    vmem = pl.BlockSpec(memory_space=pltpu.VMEM)
    result = pl.pallas_call(
        functools.partial(kernel, dims),
        out_shape=jax.ShapeDtypeStruct((bins, slots), BF16),
        in_specs=[vmem] * 6,
        out_specs=vmem,
        scratch_shapes=scratch,
        compiler_params=pltpu.CompilerParams(
            collective_id=0, has_side_effects=True, vmem_limit_bytes=60 * 1024 * 1024
        ),
        name="wave_step",
    )(masked, courant.T, upwind.T, sea, owner.reshape(lon, lc), coupling)
    return result.T.reshape(1, 1, slots, bins)


def solution(mesh):
    placed = (P("bins", "pts", None), P(), P(), P(), P("pts", None), P("pts", "bins", None, None))
    return jax.shard_map(
        local, mesh=mesh, in_specs=placed, out_specs=P("pts", "bins", None, None), check_vma=False
    )
```

```python
import functools

import jax
import jax.numpy as jnp
from jax import lax
from jax.experimental import pallas as pl
from jax.experimental.pallas import tpu as pltpu
from jax.sharding import PartitionSpec as P

MESH = pl.DeviceIdType.MESH
BF16, F32 = jnp.bfloat16, jnp.float32
NT = (((1,), (1,)), ((), ()))
LANES = 128


def dot(a, b, dims=None):
    if dims is None:
        return jnp.dot(a, b, preferred_element_type=F32)
    return lax.dot_general(a, b, dims, preferred_element_type=F32)


def far_first(count):
    steps = [(count // 2 + ((k + 1) // 2) * (1 - 2 * (k % 2))) % count for k in range(count)]
    return [s for s in steps if s]


def near_first(count):
    return far_first(count)[::-1]


def each_peer(me, count, act):
    if count != 64:
        for d in range(1, count):
            act(lax.rem(me + d, count))
        return
    y, x, core = me // 8, lax.rem(me // 2, 4), lax.rem(me, 2)
    here = [
        lax.rem(x + dx, 4) * 2 + lax.rem(core + dc, 2)
        for dx in far_first(4) + [0]
        for dc in (1, 0)
    ]

    @pl.loop(0, 7)
    def _(k):
        row = lax.rem(y + 4 + ((k + 1) // 2) * (1 - 2 * lax.rem(k, 2)) + 8, 8) * 8
        for place in here:
            act(row + place)

    for place in here[:-1]:
        act(y * 8 + place)


def plan_chunks(blocks, size):
    total = (blocks - 1) * size
    cuts = [0]
    while cuts[-1] < total:
        left = total - cuts[-1]
        step = LANES // 2 if left <= LANES // 2 else LANES if left < 2 * LANES else 2 * LANES
        cuts.append(cuts[-1] + step)
    chunks = [([(0, 0, size)], LANES)]
    for a, b in zip(cuts[:-1], cuts[1:]):
        pieces, at = [], a
        while at < min(b, total):
            v, q = at // size + 1, at % size
            n = min(size - q, b - at)
            pieces.append((v, q, n))
            at += n
        chunks.append((pieces, b - a))
    return chunks


def kernel(dims, x, courant, upwind, sea, owner, table_hbm, out, *scratch):
    np_, nb, lb, padded, chunks, lon, lc, cap, slots, bins = dims
    nk = len(chunks)
    fixed, rest = scratch[:16], scratch[16:]
    edge, hbuf, coef, sel, dbuf, acc, send, got, coupling, hss, hrs, zss, zrs, xss, xrs, cs = fixed
    gath, recv, wmat = [rest[k * nk:(k + 1) * nk] for k in range(3)]
    me = lax.axis_index("pts")
    mz = lax.axis_index("bins")
    up, down = lax.rem(me + 1, np_), lax.rem(me + np_ - 1, np_)
    lat = x.shape[2]
    pts = lon * lc
    tiles = 4
    mt = slots // tiles
    own_tiles = np_ // tiles
    full = dbuf.shape[1]
    half = LANES // 2
    distances = [0] + near_first(nb)
    groups = [(a, min(16, lb - a)) for a in range(0, padded, 16)]
    rounds = [groups[a:a + 2] for a in range(0, len(groups), 2)]

    barrier = pltpu.get_barrier_semaphore()

    def greet(peer):
        pl.semaphore_signal(barrier, inc=1, device_id={"pts": peer}, device_id_type=MESH)

    each_peer(me, np_, greet)
    for d in distances[1:]:
        pl.semaphore_signal(
            barrier, inc=1, device_id={"bins": lax.rem(mz + d, nb)}, device_id_type=MESH
        )

    for side, row in ((0, lon - 1), (1, 0)):
        edge[side, 0:lb, :] = x[row] * sea[row:row + 1, :].astype(BF16)
        if padded > lb:
            edge[side, lb:padded, :] = jnp.zeros((padded - lb, lat), BF16)
    if padded > lb:
        for j in range(nb):
            for i in range(lon):
                send[j, i, lb:padded, :] = jnp.zeros((padded - lb, lc), BF16)

    low_on = jnp.where(me > 0, 1.0, 0.0).astype(F32)
    high_on = jnp.where(me < np_ - 1, 1.0, 0.0).astype(F32)

    def line(i, a, n):
        if i < 0:
            return hbuf[0, a:a + n, :].astype(F32) * low_on
        if i == lon:
            return hbuf[1, a:a + n, :].astype(F32) * high_on
        return x[i, a:a + n, :].astype(F32) * sea[i:i + 1, :].astype(F32)

    def advect(i, a, n):
        cx, cy = coef[a:a + n, 0:1], coef[a:a + n, 1:2]
        ux, uy = coef[a:a + n, 2:3], coef[a:a + n, 3:4]
        lane = lax.broadcasted_iota(jnp.int32, (n, lat), 1)
        center = line(i, a, n)
        donor_x = jnp.where(ux == 0.0, line(i - 1, a, n), line(i + 1, a, n))
        lower = jnp.where(lane == 0, 0.0, pltpu.roll(center, 1, 1))
        higher = jnp.where(lane == lat - 1, 0.0, pltpu.roll(center, lat - 1, 1))
        donor_y = jnp.where(uy == 0.0, lower, higher)
        moved = center - cx * (center - donor_x) - cy * (center - donor_y)
        moved = (moved * sea[i:i + 1, :].astype(F32)).astype(BF16)
        for j in range(nb):
            send[j, i, a:a + n, :] = moved[:, j * lc:(j + 1) * lc]

    pl.semaphore_wait(barrier, np_ - 1 + nb - 1)

    spans = [pl.ds(g[0][0], sum(16 for _ in g)) for g in rounds]
    for r, span in enumerate(spans):
        for side, there in ((0, up), (1, down)):
            pltpu.make_async_remote_copy(
                src_ref=edge.at[side, span],
                dst_ref=hbuf.at[side, span],
                send_sem=hss.at[r],
                recv_sem=hrs.at[r],
                device_id={"pts": there},
                device_id_type=MESH,
            ).start()
    load = pltpu.make_async_copy(table_hbm, coupling, cs.at[0])
    load.start()
    first = mz * lb
    rows = lax.broadcasted_iota(jnp.int32, (padded, bins), 0)
    cols = lax.broadcasted_iota(jnp.int32, (padded, bins), 1)
    pick = jnp.where((rows < lb) & (cols == rows + first), 1.0, 0.0).astype(F32)
    table = jnp.concatenate(
        [courant[...], upwind[...].astype(F32), jnp.zeros((4, bins), F32)], axis=0
    )
    coef[:, 0:8] = lax.dot_general(
        pick, table, NT, precision=lax.Precision.HIGHEST, preferred_element_type=F32
    )

    ids = lax.broadcasted_iota(jnp.int32, (np_, lc), 0)
    named = jnp.concatenate(
        [jnp.where(ids == owner[i:i + 1, :], 1.0, 0.0) for i in range(lon)], axis=1
    )
    before = lax.broadcasted_iota(jnp.int32, (pts, pts), 0)
    after = lax.broadcasted_iota(jnp.int32, (pts, pts), 1)
    upper = jnp.where(before <= after, 1.0, 0.0).astype(BF16)
    counts = dot(named.astype(BF16), upper)
    rank = jnp.sum(counts * named, axis=0, keepdims=True) - 1.0
    column = pl.multiple_of(mz * lc, LANES)
    for i in range(lon):
        slot = owner[i:i + 1, :].astype(F32) * float(cap) + rank[:, i * lc:(i + 1) * lc]
        weight = sea[i:i + 1, pl.ds(column, lc)].astype(F32)
        row = lax.broadcasted_iota(jnp.int32, (slots, lc), 0).astype(F32)
        sel[:, i * lc:(i + 1) * lc] = jnp.where(row == slot, weight, 0.0).astype(BF16)

    for a, n in groups:
        for i in range(1, lon - 1):
            advect(i, a, n)

    def pass_on(v, span):
        there = lax.rem(mz + distances[v], nb)
        pltpu.make_async_remote_copy(
            src_ref=send.at[there, :, span],
            dst_ref=got.at[v, :, span],
            send_sem=zss.at[v],
            recv_sem=zrs.at[v],
            device_id={"bins": there},
            device_id_type=MESH,
        ).start()

    near = min(2, nb - 1)
    for r, span in enumerate(spans):
        pltpu.make_async_copy(hbuf.at[:, span], hbuf.at[:, span], hrs.at[r]).wait()
        for a, n in rounds[r]:
            advect(0, a, n)
            advect(lon - 1, a, n)
        for v in range(1, near + 1):
            pass_on(v, span)
    for v in range(near + 1, nb):
        pass_on(v, slice(None))

    here = [False] * nb

    def select(c):
        pieces, width = chunks[c]
        for v, _, _ in pieces:
            if v and not here[v]:
                here[v] = True
                pltpu.make_async_copy(got.at[v], got.at[v], zrs.at[v]).wait()

        def column_of(i):
            parts = [
                (got[v, i, q:q + n, :] if v else send[mz, i, q:q + n, :]) for v, q, n in pieces
            ]
            spare = width - sum(n for _, _, n in pieces)
            if spare:
                parts.append(jnp.zeros((spare, lc), BF16))
            if width == half:
                parts = parts + parts
            return parts[0] if len(parts) == 1 else jnp.concatenate(parts, axis=0)

        @pl.loop(0, tiles)
        def _(m):
            part = sel[pl.ds(pl.multiple_of(m * mt, mt), mt), :]
            block = jnp.concatenate([column_of(i) for i in range(lon)], axis=1)
            wide = max(width, LANES)
            rows = dot(part, block, NT).reshape(own_tiles, cap, wide)
            if width == half:
                left = lax.broadcasted_iota(jnp.int32, (own_tiles, cap // 2, wide), 2) < half
                rows = jnp.where(left, rows[:, :cap // 2], rows[:, cap // 2:])
            gath[c][pl.ds(m * own_tiles, own_tiles)] = rows.astype(BF16)

        def push(peer):
            pltpu.make_async_remote_copy(
                src_ref=gath[c].at[peer],
                dst_ref=recv[c].at[me],
                send_sem=xss.at[c],
                recv_sem=xrs.at[c],
                device_id={"pts": peer},
                device_id_type=MESH,
            ).start()

        each_peer(me, np_, push)
        pltpu.make_async_copy(gath[c].at[me], recv[c].at[me], xrs.at[c]).start()

    def bin_of(k, c):
        pieces, width = chunks[c]
        if width == half:
            k = jnp.where(k < half, k, k - half)
        at, result = 0, jnp.full(k.shape, -1, jnp.int32)
        for v, q, n in pieces:
            block = lax.rem(mz + nb - distances[v], nb) * lb
            inside = (k >= at) & (k < at + min(n, lb - q))
            result = jnp.where(inside, block + q - at + k, result)
            at += n
        return result

    def prepare(c):
        width = max(chunks[c][1], LANES)
        k = lax.broadcasted_iota(jnp.int32, (width, bins), 0)
        n = lax.broadcasted_iota(jnp.int32, (width, bins), 1)
        order = jnp.where(n == bin_of(k, c), 1.0, 0.0).astype(BF16)
        dbuf[0:width, 0:bins] = dot(order, coupling[...]).astype(BF16)
        if full > bins:
            dbuf[0:width, bins:] = jnp.zeros((width, full - bins), BF16)
        e0 = lax.broadcasted_iota(jnp.int32, (LANES, LANES), 0)
        e1 = lax.broadcasted_iota(jnp.int32, (LANES, LANES), 1)
        eye = jnp.where(e0 == e1, 1.0, 0.0).astype(BF16)
        for t in range(full // LANES):
            wmat[c][t * LANES:(t + 1) * LANES, 0:width] = dot(
                eye, dbuf[0:width, t * LANES:(t + 1) * LANES], NT
            ).astype(BF16)
        wmat[c][bins:bins + 8, 0:width] = jnp.ones((8, width), BF16)
        n = lax.broadcasted_iota(jnp.int32, (full, width), 0)
        k = lax.broadcasted_iota(jnp.int32, (full, width), 1)
        wmat[c][:, width:] = jnp.where(n == bin_of(k, c), 1.0, 0.0).astype(BF16)

    def couple(c):
        pltpu.make_async_copy(gath[c], recv[c], xrs.at[c]).wait()
        width = max(chunks[c][1], LANES)

        @pl.loop(0, tiles)
        def _(m):
            rows = recv[c][pl.ds(m * own_tiles, own_tiles)]
            if chunks[c][1] == half:
                left = lax.broadcasted_iota(jnp.int32, rows.shape, 2) < half
                none = jnp.zeros_like(rows)
                rows = jnp.concatenate(
                    [jnp.where(left, rows, none), jnp.where(left, none, rows)], axis=1
                )
            rows = rows.reshape(mt, width)
            if width == LANES:
                rows = jnp.concatenate([rows, rows], axis=1)
                total = dot(wmat[c][0:bins + 8, :], rows, NT)
            else:
                total = dot(wmat[c][0:bins + 8, 0:width], rows, NT)
                total = total + dot(wmat[c][0:bins + 8, width:], rows, NT)
            if c > 0:
                total = total + acc[m]
            if c < nk - 1:
                acc[m] = total
            else:
                scale = 1.0 / (1.0 + total[bins:bins + 1, :] / float(bins))
                out[:, pl.ds(pl.multiple_of(m * mt, mt), mt)] = (total[0:bins] * scale).astype(BF16)

    select(0)
    select(1)
    load.wait()
    prepare(0)
    prepare(1)
    for c in range(2, nk):
        select(c)
        prepare(c)
        couple(c - 2)
    couple(nk - 2)
    couple(nk - 1)
    for r, span in enumerate(spans):
        pltpu.make_async_copy(edge.at[:, span], hbuf.at[:, span], hss.at[r]).wait()
    for v in range(1, nb):
        pltpu.make_async_copy(send.at[v], got.at[v], zss.at[v]).wait()
    for c in range(nk):
        pltpu.make_async_copy(
            gath[c].at[pl.ds(0, np_ - 1)], recv[c].at[pl.ds(0, np_ - 1)], xss.at[c]
        ).wait()


def local(spectrum, courant, upwind, coupling, sea, owner):
    lb, lon, lat = spectrum.shape
    np_, nb = lax.axis_size("pts"), lax.axis_size("bins")
    bins = coupling.shape[0]
    lc = lat // nb
    pts = lon * lc
    cap = max(2, (2 * pts + np_ - 1) // np_)
    slots = np_ * cap
    padded = -(-lb // 16) * 16
    chunks = plan_chunks(nb, lb)
    nk = len(chunks)
    full = -(-(bins + 8) // LANES) * LANES
    dims = (np_, nb, lb, padded, chunks, lon, lc, cap, slots, bins)
    most = max(LANES, max(w for _, w in chunks))
    scratch = [
        pltpu.VMEM((2, padded, lat), BF16),
        pltpu.VMEM((2, padded, lat), BF16),
        pltpu.VMEM((padded, LANES), F32),
        pltpu.VMEM((slots, pts), BF16),
        pltpu.VMEM((most, full), BF16),
        pltpu.VMEM((4, bins + 8, slots // 4), F32),
        pltpu.VMEM((nb, lon, padded, lc), BF16),
        pltpu.VMEM((nb, lon, padded, lc), BF16),
        pltpu.VMEM((bins, bins), BF16),
    ]
    counts = [-(-padded // 32)] * 2 + [nb] * 2 + [nk] * 2 + [1]
    scratch += [pltpu.SemaphoreType.DMA((n,)) for n in counts]
    packed = [(np_, cap if w >= LANES else cap // 2, max(w, LANES)) for _, w in chunks]
    scratch += [pltpu.VMEM(s, BF16) for s in packed] * 2
    scratch += [pltpu.VMEM((full, 2 * max(w, LANES)), BF16) for _, w in chunks]
    vmem = pl.BlockSpec(memory_space=pltpu.VMEM)
    result = pl.pallas_call(
        functools.partial(kernel, dims),
        out_shape=jax.ShapeDtypeStruct((bins, slots), BF16),
        in_specs=[vmem] * 5 + [pl.BlockSpec(memory_space=pltpu.HBM)],
        out_specs=vmem,
        scratch_shapes=scratch,
        compiler_params=pltpu.CompilerParams(
            collective_id=0, has_side_effects=True, vmem_limit_bytes=50 * 1024 * 1024
        ),
        name="wave_step",
    )(jnp.transpose(spectrum, (1, 0, 2)), courant.T, upwind.T, sea, owner.reshape(lon, lc), coupling)
    return result.T.reshape(1, 1, slots, bins)


def solution(mesh):
    placed = (P("bins", "pts", None), P(), P(), P(), P("pts", None), P("pts", "bins", None, None))
    return jax.shard_map(
        local, mesh=mesh, in_specs=placed, out_specs=P("pts", "bins", None, None), check_vma=False
    )
```

```python
import functools

import jax
import jax.numpy as jnp
from jax import lax
from jax.experimental import pallas as pl
from jax.experimental.pallas import tpu as pltpu
from jax.sharding import PartitionSpec as P

MESH = pl.DeviceIdType.MESH
BF16, F32 = jnp.bfloat16, jnp.float32
NT = (((1,), (1,)), ((), ()))
LANES = 128


def dot(a, b, dims=None):
    if dims is None:
        return jnp.dot(a, b, preferred_element_type=F32)
    return lax.dot_general(a, b, dims, preferred_element_type=F32)


def far_first(count):
    steps = [(count // 2 + ((k + 1) // 2) * (1 - 2 * (k % 2))) % count for k in range(count)]
    return [s for s in steps if s]


def near_first(count):
    return far_first(count)[::-1]


def each_peer(me, count, act):
    if count != 64:
        for d in range(1, count):
            act(lax.rem(me + d, count))
        return
    y, x, core = me // 8, lax.rem(me // 2, 4), lax.rem(me, 2)
    here = [
        lax.rem(x + dx, 4) * 2 + lax.rem(core + dc, 2)
        for dx in far_first(4) + [0]
        for dc in (1, 0)
    ]

    @pl.loop(0, 7)
    def _(k):
        row = lax.rem(y + 4 + ((k + 1) // 2) * (1 - 2 * lax.rem(k, 2)) + 8, 8) * 8
        for place in here:
            act(row + place)

    for place in here[:-1]:
        act(y * 8 + place)


def plan_chunks(blocks, size):
    total = (blocks - 2) * size
    cuts = [0]
    while cuts[-1] < total:
        left = total - cuts[-1]
        step = LANES // 2 if left <= LANES // 2 else LANES if left < 2 * LANES or len(cuts) < 3 else 2 * LANES
        cuts.append(cuts[-1] + step)
    chunks = [([(0, 0, size)], LANES)]
    for a, b in zip(cuts[:-1], cuts[1:]):
        pieces, at = [], a
        while at < min(b, total):
            v, q = at // size + 1, at % size
            n = min(size - q, b - at)
            pieces.append((v, q, n))
            at += n
        chunks.append((pieces, b - a))
    return chunks + [([(blocks - 1, 0, size)], LANES)]


def kernel(dims, x, courant, upwind, sea, owner, table_hbm, out, *scratch):
    np_, nb, lb, padded, chunks, lon, lc, cap, slots, bins = dims
    nk = len(chunks)
    fixed, rest = scratch[:16], scratch[16:]
    edge, hbuf, coef, sel, dbuf, acc, send, got, coupling, hss, hrs, zss, zrs, xss, xrs, cs = fixed
    gath, recv, wmat = [rest[k * nk:(k + 1) * nk] for k in range(3)]
    me = lax.axis_index("pts")
    mz = lax.axis_index("bins")
    up, down = lax.rem(me + 1, np_), lax.rem(me + np_ - 1, np_)
    lat = x.shape[2]
    pts = lon * lc
    tiles = 4
    mt = slots // tiles
    own_tiles = np_ // tiles
    full = dbuf.shape[1]
    half = LANES // 2
    distances = [0] + near_first(nb)
    groups = [(a, min(16, lb - a)) for a in range(0, padded, 16)]
    rounds = [groups[a:a + 2] for a in range(0, len(groups), 2)]

    barrier = pltpu.get_barrier_semaphore()

    def greet(peer):
        pl.semaphore_signal(barrier, inc=1, device_id={"pts": peer}, device_id_type=MESH)

    each_peer(me, np_, greet)
    for d in distances[1:]:
        pl.semaphore_signal(
            barrier, inc=1, device_id={"bins": lax.rem(mz + d, nb)}, device_id_type=MESH
        )

    for side, row in ((0, lon - 1), (1, 0)):
        edge[side, 0:lb, :] = x[row] * sea[row:row + 1, :].astype(BF16)
        if padded > lb:
            edge[side, lb:padded, :] = jnp.zeros((padded - lb, lat), BF16)
    if padded > lb:
        for j in range(nb):
            for i in range(lon):
                send[j, i, lb:padded, :] = jnp.zeros((padded - lb, lc), BF16)

    low_on = jnp.where(me > 0, 1.0, 0.0).astype(F32)
    high_on = jnp.where(me < np_ - 1, 1.0, 0.0).astype(F32)

    def line(i, a, n):
        if i < 0:
            return hbuf[0, a:a + n, :].astype(F32) * low_on
        if i == lon:
            return hbuf[1, a:a + n, :].astype(F32) * high_on
        return x[i, a:a + n, :].astype(F32) * sea[i:i + 1, :].astype(F32)

    def advect(i, a, n):
        cx, cy = coef[a:a + n, 0:1], coef[a:a + n, 1:2]
        ux, uy = coef[a:a + n, 2:3], coef[a:a + n, 3:4]
        lane = lax.broadcasted_iota(jnp.int32, (n, lat), 1)
        center = line(i, a, n)
        donor_x = jnp.where(ux == 0.0, line(i - 1, a, n), line(i + 1, a, n))
        lower = jnp.where(lane == 0, 0.0, pltpu.roll(center, 1, 1))
        higher = jnp.where(lane == lat - 1, 0.0, pltpu.roll(center, lat - 1, 1))
        donor_y = jnp.where(uy == 0.0, lower, higher)
        moved = center - cx * (center - donor_x) - cy * (center - donor_y)
        moved = (moved * sea[i:i + 1, :].astype(F32)).astype(BF16)
        for j in range(nb):
            send[j, i, a:a + n, :] = moved[:, j * lc:(j + 1) * lc]

    pl.semaphore_wait(barrier, np_ - 1 + nb - 1)

    spans = [pl.ds(g[0][0], sum(16 for _ in g)) for g in rounds]
    for r, span in enumerate(spans):
        for side, there in ((0, up), (1, down)):
            pltpu.make_async_remote_copy(
                src_ref=edge.at[side, span],
                dst_ref=hbuf.at[side, span],
                send_sem=hss.at[r],
                recv_sem=hrs.at[r],
                device_id={"pts": there},
                device_id_type=MESH,
            ).start()
    load = pltpu.make_async_copy(table_hbm, coupling, cs.at[0])
    load.start()
    first = mz * lb
    rows = lax.broadcasted_iota(jnp.int32, (padded, bins), 0)
    cols = lax.broadcasted_iota(jnp.int32, (padded, bins), 1)
    pick = jnp.where((rows < lb) & (cols == rows + first), 1.0, 0.0).astype(F32)
    table = jnp.concatenate(
        [courant[...], upwind[...].astype(F32), jnp.zeros((4, bins), F32)], axis=0
    )
    coef[:, 0:8] = lax.dot_general(
        pick, table, NT, precision=lax.Precision.HIGHEST, preferred_element_type=F32
    )

    ids = lax.broadcasted_iota(jnp.int32, (np_, lc), 0)
    named = jnp.concatenate(
        [jnp.where(ids == owner[i:i + 1, :], 1.0, 0.0) for i in range(lon)], axis=1
    )
    before = lax.broadcasted_iota(jnp.int32, (pts, pts), 0)
    after = lax.broadcasted_iota(jnp.int32, (pts, pts), 1)
    upper = jnp.where(before <= after, 1.0, 0.0).astype(BF16)
    counts = dot(named.astype(BF16), upper)
    rank = jnp.sum(counts * named, axis=0, keepdims=True) - 1.0
    column = pl.multiple_of(mz * lc, LANES)
    for i in range(lon):
        slot = owner[i:i + 1, :].astype(F32) * float(cap) + rank[:, i * lc:(i + 1) * lc]
        weight = sea[i:i + 1, pl.ds(column, lc)].astype(F32)
        row = lax.broadcasted_iota(jnp.int32, (slots, lc), 0).astype(F32)
        sel[:, i * lc:(i + 1) * lc] = jnp.where(row == slot, weight, 0.0).astype(BF16)

    for a, n in groups:
        for i in range(1, lon - 1):
            advect(i, a, n)

    def pass_on(v, span):
        there = lax.rem(mz + distances[v], nb)
        pltpu.make_async_remote_copy(
            src_ref=send.at[there, :, span],
            dst_ref=got.at[v, :, span],
            send_sem=zss.at[v],
            recv_sem=zrs.at[v],
            device_id={"bins": there},
            device_id_type=MESH,
        ).start()

    near = min(2, nb - 1)
    for r, span in enumerate(spans):
        pltpu.make_async_copy(hbuf.at[:, span], hbuf.at[:, span], hrs.at[r]).wait()
        for a, n in rounds[r]:
            advect(0, a, n)
            advect(lon - 1, a, n)
        for v in range(1, near + 1):
            pass_on(v, span)
    for v in range(near + 1, nb):
        pass_on(v, slice(None))

    here = [False] * nb

    def select(c):
        pieces, width = chunks[c]
        for v, _, _ in pieces:
            if v and not here[v]:
                here[v] = True
                pltpu.make_async_copy(got.at[v], got.at[v], zrs.at[v]).wait()

        def column_of(i):
            parts = [
                (got[v, i, q:q + n, :] if v else send[mz, i, q:q + n, :]) for v, q, n in pieces
            ]
            spare = width - sum(n for _, _, n in pieces)
            if spare:
                parts.append(jnp.zeros((spare, lc), BF16))
            if width == half:
                parts = parts + parts
            return parts[0] if len(parts) == 1 else jnp.concatenate(parts, axis=0)

        @pl.loop(0, tiles)
        def _(m):
            part = sel[pl.ds(pl.multiple_of(m * mt, mt), mt), :]
            block = jnp.concatenate([column_of(i) for i in range(lon)], axis=1)
            wide = max(width, LANES)
            rows = dot(part, block, NT).reshape(own_tiles, cap, wide)
            if width == half:
                left = lax.broadcasted_iota(jnp.int32, (own_tiles, cap // 2, wide), 2) < half
                rows = jnp.where(left, rows[:, :cap // 2], rows[:, cap // 2:])
            gath[c][pl.ds(m * own_tiles, own_tiles)] = rows.astype(BF16)

        def push(peer):
            pltpu.make_async_remote_copy(
                src_ref=gath[c].at[peer],
                dst_ref=recv[c].at[me],
                send_sem=xss.at[c],
                recv_sem=xrs.at[c],
                device_id={"pts": peer},
                device_id_type=MESH,
            ).start()

        each_peer(me, np_, push)
        pltpu.make_async_copy(gath[c].at[me], recv[c].at[me], xrs.at[c]).start()

    def bin_of(k, c):
        pieces, width = chunks[c]
        if width == half:
            k = jnp.where(k < half, k, k - half)
        at, result = 0, jnp.full(k.shape, -1, jnp.int32)
        for v, q, n in pieces:
            block = lax.rem(mz + nb - distances[v], nb) * lb
            inside = (k >= at) & (k < at + min(n, lb - q))
            result = jnp.where(inside, block + q - at + k, result)
            at += n
        return result

    def prepare(c):
        width = max(chunks[c][1], LANES)
        k = lax.broadcasted_iota(jnp.int32, (width, bins), 0)
        n = lax.broadcasted_iota(jnp.int32, (width, bins), 1)
        order = jnp.where(n == bin_of(k, c), 1.0, 0.0).astype(BF16)
        dbuf[0:width, 0:bins] = dot(order, coupling[...]).astype(BF16)
        if full > bins:
            dbuf[0:width, bins:] = jnp.zeros((width, full - bins), BF16)
        e0 = lax.broadcasted_iota(jnp.int32, (LANES, LANES), 0)
        e1 = lax.broadcasted_iota(jnp.int32, (LANES, LANES), 1)
        eye = jnp.where(e0 == e1, 1.0, 0.0).astype(BF16)
        for t in range(full // LANES):
            wmat[c][t * LANES:(t + 1) * LANES, 0:width] = dot(
                eye, dbuf[0:width, t * LANES:(t + 1) * LANES], NT
            ).astype(BF16)
        wmat[c][bins:bins + 8, 0:width] = jnp.ones((8, width), BF16)
        n = lax.broadcasted_iota(jnp.int32, (full, width), 0)
        k = lax.broadcasted_iota(jnp.int32, (full, width), 1)
        wmat[c][:, width:] = jnp.where(n == bin_of(k, c), 1.0, 0.0).astype(BF16)

    def couple(c):
        pltpu.make_async_copy(gath[c], recv[c], xrs.at[c]).wait()
        width = max(chunks[c][1], LANES)

        @pl.loop(0, tiles)
        def _(m):
            rows = recv[c][pl.ds(m * own_tiles, own_tiles)]
            if chunks[c][1] == half:
                left = lax.broadcasted_iota(jnp.int32, rows.shape, 2) < half
                none = jnp.zeros_like(rows)
                rows = jnp.concatenate(
                    [jnp.where(left, rows, none), jnp.where(left, none, rows)], axis=1
                )
            rows = rows.reshape(mt, width)
            if width == LANES:
                rows = jnp.concatenate([rows, rows], axis=1)
                total = dot(wmat[c][0:bins + 8, :], rows, NT)
            else:
                total = dot(wmat[c][0:bins + 8, 0:width], rows, NT)
                total = total + dot(wmat[c][0:bins + 8, width:], rows, NT)
            if c > 0:
                total = total + acc[m]
            if c < nk - 1:
                acc[m] = total
            else:
                scale = 1.0 / (1.0 + total[bins:bins + 1, :] / float(bins))
                out[:, pl.ds(pl.multiple_of(m * mt, mt), mt)] = (total[0:bins] * scale).astype(BF16)

    select(0)
    select(1)
    select(2)
    load.wait()
    for c in range(3):
        prepare(c)
    for c in range(3, nk):
        select(c)
        prepare(c)
        if c == 3:
            couple(0)
        couple(c - 2)
    couple(nk - 2)
    couple(nk - 1)
    for r, span in enumerate(spans):
        pltpu.make_async_copy(edge.at[:, span], hbuf.at[:, span], hss.at[r]).wait()
    for v in range(1, nb):
        pltpu.make_async_copy(send.at[v], got.at[v], zss.at[v]).wait()
    for c in range(nk):
        pltpu.make_async_copy(
            gath[c].at[pl.ds(0, np_ - 1)], recv[c].at[pl.ds(0, np_ - 1)], xss.at[c]
        ).wait()


def local(spectrum, courant, upwind, coupling, sea, owner):
    lb, lon, lat = spectrum.shape
    np_, nb = lax.axis_size("pts"), lax.axis_size("bins")
    bins = coupling.shape[0]
    lc = lat // nb
    pts = lon * lc
    cap = max(2, (2 * pts + np_ - 1) // np_)
    slots = np_ * cap
    padded = -(-lb // 16) * 16
    chunks = plan_chunks(nb, lb)
    nk = len(chunks)
    full = -(-(bins + 8) // LANES) * LANES
    dims = (np_, nb, lb, padded, chunks, lon, lc, cap, slots, bins)
    most = max(LANES, max(w for _, w in chunks))
    scratch = [
        pltpu.VMEM((2, padded, lat), BF16),
        pltpu.VMEM((2, padded, lat), BF16),
        pltpu.VMEM((padded, LANES), F32),
        pltpu.VMEM((slots, pts), BF16),
        pltpu.VMEM((most, full), BF16),
        pltpu.VMEM((4, bins + 8, slots // 4), F32),
        pltpu.VMEM((nb, lon, padded, lc), BF16),
        pltpu.VMEM((nb, lon, padded, lc), BF16),
        pltpu.VMEM((bins, bins), BF16),
    ]
    counts = [-(-padded // 32)] * 2 + [nb] * 2 + [nk] * 2 + [1]
    scratch += [pltpu.SemaphoreType.DMA((n,)) for n in counts]
    packed = [(np_, cap if w >= LANES else cap // 2, max(w, LANES)) for _, w in chunks]
    scratch += [pltpu.VMEM(s, BF16) for s in packed] * 2
    scratch += [pltpu.VMEM((full, 2 * max(w, LANES)), BF16) for _, w in chunks]
    vmem = pl.BlockSpec(memory_space=pltpu.VMEM)
    result = pl.pallas_call(
        functools.partial(kernel, dims),
        out_shape=jax.ShapeDtypeStruct((bins, slots), BF16),
        in_specs=[vmem] * 5 + [pl.BlockSpec(memory_space=pltpu.HBM)],
        out_specs=vmem,
        scratch_shapes=scratch,
        compiler_params=pltpu.CompilerParams(
            collective_id=0, has_side_effects=True, vmem_limit_bytes=50 * 1024 * 1024
        ),
        name="wave_step",
    )(jnp.transpose(spectrum, (1, 0, 2)), courant.T, upwind.T, sea, owner.reshape(lon, lc), coupling)
    return result.T.reshape(1, 1, slots, bins)


def solution(mesh):
    placed = (P("bins", "pts", None), P(), P(), P(), P("pts", None), P("pts", "bins", None, None))
    return jax.shard_map(
        local, mesh=mesh, in_specs=placed, out_specs=P("pts", "bins", None, None), check_vma=False
    )
```
